128 devices in a mesh: section: 2 (over x_lo), tm: 8 (over x_hi, y), mp: 8 (over z, core).
Axes of the slice: x: 4 (x_hi: 2, x_lo: 2; x = x_hi * 2 + x_lo), y: 4, z: 4, core: 2. Of those that a mesh axis runs over, the one named last changes fastest.
Arguments:
- frame_len: int32 [8], replicated, may hold values from 128 to 512, as said below
- slot_utt: int32 [16], replicated, may hold values from -1 to 7, as said below
- enc_in: bfloat16 [512, 8, 1280], P(('section', 'tm')), may hold values from -42 to 42
- ffn_up: bfloat16 [1280, 5120], P(None, 'mp'), may hold values from -0.15625 to 0.15625
- ffn_down: bfloat16 [5120, 1280], P('mp'), may hold values from -0.078125 to 0.078125
- kv_proj: bfloat16 [1280, 1024], replicated, may hold values from -10 to 10
- hyp_state: bfloat16 [16, 8, 16, 4096], P('tm'), may hold values from -37 to 37
- hyp_tok: int32 [16, 8, 16], P('tm'), may hold values from 0 to 63999
- hyp_len: int32 [16, 8], P('tm'), may hold values from 1 to 16
- q_proj: bfloat16 [4096, 4096], P(None, ('section', 'mp')), may hold values from -0.75 to 0.75
- o_proj: bfloat16 [4096, 4096], P(('section', 'mp')), may hold values from -1 to 1
- head: bfloat16 [64000, 4096], P(('section', 'tm', 'mp')), may hold values from -45 to 45
Outputs:
- hyp_scores: float32 [16, 8], P('tm')
The draws below stay inside these ranges and needn't reach their ends.
Inputs may be any that keep to these rules, and one draw needn't show every extreme that they name: `frame_len`: one utterance in every draw has all 512 frames. `slot_utt`: every one of the 8 utterances sits in exactly one slot; slots g * 2 to (g + 1) * 2 - 1 belong to group g, and at least one group has all 2 slots filled.
All inputs are finite; a program needn't handle non-finite values.
Results may differ from the reference program's by a relative error of at most 0.005.
The reference program's roundings to bfloat16 on the way count: a program that leaves them out, or rounds other values in their place, can miss the bound.
Values may be sent and summed in bfloat16 or wider, within the bound.
A program may use at most 128 MiB of HBM per device.

```python
import math
import jax
import jax.numpy as jnp
import numpy as np
from jax import lax

D = 4096
NH = 32
KVH = 4
HD = 128
V = 64000
DE = 1280
EFF = 5120
HYP = 8
HLEN = 16
UMAX = 2
U = 8
SLOTS = 16
FRAMES = 512


def log_scales(key, count, low, high):
    return jnp.exp(jax.random.uniform(key, (count,), jnp.float32, math.log(low), math.log(high)))


def draw_frame_len(key, part):
    keys = jax.random.split(jax.random.fold_in(key, 11), 2)
    lengths = jax.random.randint(keys[0], (U,), FRAMES // 4, FRAMES + 1)
    longest = jax.random.randint(keys[1], (), 0, U)
    return jnp.where(jnp.arange(U) == longest, FRAMES, lengths).astype(jnp.int32)


def draw_slot_utt(key, part):
    keys = jax.random.split(jax.random.fold_in(key, 23), 3)
    priority = jax.random.permutation(keys[0], SLOTS)
    filled = jax.random.randint(keys[1], (), 0, SLOTS // UMAX)
    slot_ids = jnp.arange(SLOTS)
    priority = jnp.where(slot_ids // UMAX == filled, -1 - slot_ids % UMAX, priority)
    ranking = jnp.argsort(jnp.argsort(priority, stable=True), stable=True)
    ordering = jax.random.permutation(keys[2], U)
    return jnp.where(ranking < U, ordering[jnp.minimum(ranking, U - 1)], -1).astype(jnp.int32)


def draw_enc_in(key, part):
    keys = jax.random.split(jax.random.fold_in(key, 101), 3)
    row_scale = log_scales(keys[0], FRAMES * U, 1.0, 3.2).reshape(FRAMES, U, 1)
    col_scale = log_scales(keys[1], DE, 1.0, 3.2)
    base = jnp.clip(jax.random.normal(keys[2], (FRAMES, U, DE), jnp.float32), -4.0, 4.0)
    return (base * row_scale * col_scale).astype(jnp.bfloat16)


def draw_hyp_state(key, part):
    keys = jax.random.split(jax.random.fold_in(key, 131), 3)
    row_scale = log_scales(keys[0], SLOTS * HYP * HLEN, 0.3, 3.0).reshape(SLOTS, HYP, HLEN, 1)
    col_scale = log_scales(keys[1], D, 0.3, 3.0)
    base = jnp.clip(jax.random.normal(keys[2], (SLOTS, HYP, HLEN, D), jnp.float32), -4.0, 4.0)
    return (base * row_scale * col_scale).astype(jnp.bfloat16)


def draw_kv_proj(key, part):
    keys = jax.random.split(jax.random.fold_in(key, 151), 1)
    columns = 2 * KVH * HD
    base = jnp.clip(jax.random.normal(keys[0], (DE, columns), jnp.float32), -4.0, 4.0)
    return (base / math.sqrt(DE)).astype(jnp.bfloat16)


def draw_head(key, part):
    keys = jax.random.split(jax.random.fold_in(key, 171), 1)
    scale = 3.5 / math.sqrt(D)
    base = jnp.clip(jax.random.normal(keys[0], (V, D), jnp.float32), -4.0, 4.0)
    return (base * scale).astype(jnp.bfloat16)


def with_ends(entries, own_key, least, top_value):
    spot = [jax.random.randint(jax.random.fold_in(own_key, axis), (), 0, length) for axis, length in enumerate(entries.shape)]
    main_axis = entries.shape.index(max(entries.shape))
    next_to = spot[:main_axis] + [(spot[main_axis] + 1) % entries.shape[main_axis]] + spot[main_axis + 1:]
    return entries.at[tuple(spot)].set(least).at[tuple(next_to)].set(top_value)


def level_of(rng, extent, pieces, low, largest):
    def one(dim, blocks):
        draws = jax.random.uniform(jax.random.fold_in(jax.random.fold_in(rng, 6), dim), (blocks,), jnp.float32, low / len(pieces), largest / len(pieces))
        return jnp.repeat(jnp.exp(draws), extent[dim] // blocks).reshape((-1,) + (1,) * (len(extent) - dim - 1))

    gain = one(*pieces[0])
    for cut in pieces[1:]:
        gain = gain * one(*cut)
    return gain


def rank_bounds(count, lean):
    weights = [(1 << 20) // math.isqrt(grade ** lean) + 1 for grade in range(1, count + 1)]
    width = 1 + sum(weights) // (1 << 30)
    return np.cumsum(np.array([max(1, weight // width) for weight in weights]))


def ranked_ids(own_key, shape, count, lean):
    listing = rank_bounds(count, lean)
    pick = jax.random.randint(jax.random.fold_in(own_key, 1), shape, 0, int(listing[count - 1]))
    rank = jnp.searchsorted(jnp.asarray(listing, jnp.int32), pick, side="right")
    return jax.random.permutation(jax.random.fold_in(own_key, 2), count)[rank].astype(jnp.int32)


def centred(own_key, extent, deviation, limit, cuts=(), held_as=jnp.bfloat16):
    values = jax.random.normal(own_key, extent, jnp.float32) * deviation
    if len(cuts) > 0:
        values = level_of(own_key, extent, cuts, -0.22, 0.18) * values
    return jnp.clip(values, min=-limit, max=limit).astype(held_as)


def setup_inputs(seed: int = 0) -> dict:
    seeds = jax.random.split(jax.random.key(seed), 13)
    frame_len = draw_frame_len(jax.random.fold_in(seeds[12], 71), 0)
    slot_utt = draw_slot_utt(jax.random.fold_in(seeds[12], 71), 0)
    enc_in = draw_enc_in(jax.random.fold_in(seeds[12], 71), 0)
    ffn_up = centred(seeds[3], (DE, EFF), DE ** -0.5, 0.15625, ((1, 8),))
    ffn_down = centred(seeds[4], (EFF, DE), EFF ** -0.5, 0.078125, ((0, 8),))
    kv_proj = draw_kv_proj(jax.random.fold_in(seeds[12], 71), 0)
    hyp_state = draw_hyp_state(jax.random.fold_in(seeds[12], 71), 0)
    hyp_tok = with_ends(ranked_ids(seeds[7], (SLOTS, HYP, HLEN), V, 2), jax.random.fold_in(seeds[7], 3), 0, V - 1).astype(jnp.int32)
    hyp_len = with_ends(jax.random.randint(seeds[8], (SLOTS, HYP), 1, HLEN + 1), jax.random.fold_in(seeds[8], 1), 1, HLEN).astype(jnp.int32)
    q_proj = centred(seeds[9], (D, NH * HD), 0.047, 0.75, ((1, 16),))
    o_proj = centred(seeds[10], (NH * HD, D), 0.0625, 1.0, ((0, 16),))
    head = draw_head(jax.random.fold_in(seeds[12], 71), 0)
    return {"frame_len": frame_len, "slot_utt": slot_utt, "enc_in": enc_in, "ffn_up": ffn_up, "ffn_down": ffn_down, "kv_proj": kv_proj, "hyp_state": hyp_state, "hyp_tok": hyp_tok, "hyp_len": hyp_len, "q_proj": q_proj, "o_proj": o_proj, "head": head}


def layer_norm(values):
    center = values - lax.optimization_barrier(jnp.mean(values, axis=-1, keepdims=True))
    spread = lax.optimization_barrier(jnp.mean(center * center, axis=-1, keepdims=True))
    return center * lax.rsqrt(spread + 1e-05)

def square_norm(values):
    return values * lax.rsqrt(lax.optimization_barrier(jnp.mean(values * values, axis=-1, keepdims=True)) + 1e-06)

def rounded(values):
    return lax.optimization_barrier(values.astype(jnp.bfloat16))

def reference(frame_len, slot_utt, enc_in, ffn_up, ffn_down, kv_proj, hyp_state, hyp_tok, hyp_len, q_proj, o_proj, head):
    enc_flat = enc_in.reshape(FRAMES * U, DE)
    enc_normed = layer_norm(enc_flat.astype(jnp.float32)).astype(jnp.bfloat16)
    enc_inner = jax.nn.gelu(jnp.dot(enc_normed, ffn_up, preferred_element_type=jnp.float32), approximate=False).astype(jnp.bfloat16)
    enc_mid = enc_flat.astype(jnp.float32) + jnp.dot(enc_inner, ffn_down, preferred_element_type=jnp.float32)
    enc_states = layer_norm(enc_mid).astype(jnp.bfloat16)
    keys_values = jnp.dot(enc_states, kv_proj, preferred_element_type=jnp.float32).astype(jnp.bfloat16)
    keys_values = keys_values.reshape(FRAMES, U, 2, KVH, HD)
    group_heads = NH // KVH

    def one_slot(inputs):
        states, tokens, lengths, utterance = inputs
        chosen = jnp.maximum(utterance, 0).astype(jnp.int32)
        slot_kv = lax.dynamic_index_in_dim(keys_values, chosen, 1, keepdims=False).astype(jnp.float32)
        dec_rows = states.reshape(HYP * HLEN, D).astype(jnp.float32)
        queries = rounded(jnp.dot(square_norm(dec_rows).astype(jnp.bfloat16), q_proj, preferred_element_type=jnp.float32))
        queries = queries.astype(jnp.float32).reshape(HYP * HLEN, KVH, group_heads, HD)
        scores = jnp.einsum('qkgd,fkd->kgqf', queries, slot_kv[:, 0]) / math.sqrt(HD)
        visible = jnp.arange(FRAMES, dtype=jnp.int32) < frame_len[chosen]
        scores = jnp.where(visible[None, None, None, :], scores, -jnp.inf)
        weights = rounded(jax.nn.softmax(scores, axis=-1)).astype(jnp.float32)
        context = rounded(jnp.einsum('kgqf,fkd->qkgd', weights, slot_kv[:, 1])).reshape(HYP * HLEN, NH * HD)
        resid = dec_rows + jnp.dot(context, o_proj, preferred_element_type=jnp.float32)
        out_normed = square_norm(resid).astype(jnp.bfloat16)
        logits = jnp.dot(out_normed, head.T, preferred_element_type=jnp.float32)
        picked = jnp.take_along_axis(logits, tokens.reshape(HYP * HLEN, 1).astype(jnp.int32), axis=1)[:, 0]
        token_logp = (picked - jax.scipy.special.logsumexp(logits, axis=1)).reshape(HYP, HLEN)
        valid = jnp.arange(HLEN, dtype=jnp.int32)[None, :] < lengths[:, None]
        summed = lax.optimization_barrier(jnp.sum(jnp.where(valid, token_logp, 0.0), axis=-1)) / lengths.astype(jnp.float32) + math.log(V)
        return jnp.where(utterance >= 0, summed, jnp.zeros_like(summed))
    return lax.map(one_slot, (hyp_state, hyp_tok, hyp_len, slot_utt))
```

```python
import functools
import math

import jax
import jax.numpy as jnp
from jax import lax
from jax.experimental import pallas as pl
from jax.experimental.pallas import tpu as pltpu
from jax.sharding import PartitionSpec as P

NH = 32
KVH = 4
HD = 128
V = 64000
F32 = jnp.float32
BF16 = jnp.bfloat16
MESH = pl.DeviceIdType.MESH
VMEM_LIMIT = 64000 * 1024


def position():
    section = lax.axis_index("section")
    tm = lax.axis_index("tm")
    mp = lax.axis_index("mp")
    x = lax.div(tm, 4) * 2 + section
    y = lax.rem(tm, 4)
    z = lax.div(mp, 2)
    c = lax.rem(mp, 2)
    return section, tm, mp, x, y, z, c


def device(x, y, z, c):
    return (lax.rem(x, 2), lax.div(x, 2) * 4 + y, z * 2 + c)


def around(value, step):
    return lax.rem(value + step + 4, 4)


def remote(src, dst, send_sem, recv_sem, target):
    return pltpu.make_async_remote_copy(
        src_ref=src,
        dst_ref=dst,
        send_sem=send_sem,
        recv_sem=recv_sem,
        device_id=target,
        device_id_type=MESH,
    )


def dot_nt(a, b):
    return lax.dot_general(a, b, (((1,), (1,)), ((), ())), preferred_element_type=F32)


def dot_nn(a, b):
    return jnp.dot(a, b, preferred_element_type=F32)


def normed(values):
    center = values - jnp.mean(values, axis=-1, keepdims=True)
    spread = jnp.mean(center * center, axis=-1, keepdims=True)
    return center * lax.rsqrt(spread + 1e-05)


def gelu(values):
    return 0.5 * values * (1.0 + lax.erf(values * (1.0 / math.sqrt(2.0))))


ORDERS = ((2, 1, 0), (0, 2, 1), (1, 0, 2))
WAVES = (((0, 384), (384, 384), (768, 256)), ((1024, 384), (1408, 256), (1664, 384)))

QS = (0, 1, -1, 2)
STEPS = (1, -1, 2)
UPWARD = (0, -1)
LAG = 0
SCHEDULE = tuple(
    (w, n - w * LAG) for n in range(7 + LAG) for w in range(2) if 0 <= n - w * LAG < 7 - 2 * w
)


def kernel(
    slot_ref, length_ref, tgt_ref, enc_hbm, up_hbm, down_hbm, hyp_hbm, qp_hbm, kvp_hbm, op_hbm, head_hbm,
    out_ref,
    enc_ref, up_ref, down_ref, hyp_ref, qp_ref, kvp_ref, op_ref, head,
    inner, e_core_send, e_core_recv, e_own, e_send, e_recv, kv_send, kv_all,
    dec_n, q_send, q_recv, r_send, r_recv, t_recv, targets,
    context, core_send, core_recv, own, rs_send, rs_recv, sq_send, sq_recv,
    hidden, acc, stats, all_mp, all_y, all_x,
    load, ec_s, ec_r, e_s, e_r, kv1_s, kv1_r, kv2_s, kv2_r, q_s, q_r, r_s, r_r, t_s, t_r,
    c_s, c_r, rs_s, rs_r, sq_s, sq_r, g_s, g_r, f_s, f_r, mp_s, mp_r, y_s, y_r, x_s, x_r,
):
    section, tm, mp, x, y, z, c = position()
    me = (x, y, z)
    loads = []
    for n, (source, place) in enumerate((
        (enc_hbm, enc_ref), (up_hbm, up_ref), (down_hbm, down_ref), (hyp_hbm, hyp_ref),
        (qp_hbm, qp_ref), (kvp_hbm, kvp_ref), (op_hbm, op_ref), (head_hbm, head),
    )):
        copy = pltpu.make_async_copy(source, place, load.at[n])
        copy.start()
        loads.append(copy)
    enc_load, up_load, down_load, hyp_load, qp_load, kvp_load, op_load, head_load = loads

    def neighbour(axis, step):
        place = list(me)
        place[axis] = around(place[axis], step)
        return device(place[0], place[1], place[2], c)

    partner = (section, tm, z * 2 + 1 - c)
    quad = lax.div(mp, 4)
    seat = lax.rem(mp, 4)

    barrier = pltpu.get_barrier_semaphore()
    sources = [(section, tm, lax.rem(mp + d, 8)) for d in range(1, 8)]
    sources += [(section, lax.rem(tm + d, 8), mp) for d in range(1, 8)]
    sources += [neighbour(0, 1), neighbour(0, -1)]
    sources += [(1 - section, tm, around(z, d) * 2 + c) for d in range(1, 4)]
    for target in sources:
        pl.semaphore_signal(barrier, inc=1, device_id=target, device_id_type=MESH)
    for s in range(2):
        for h in range(2):
            source_tm = h * 4 + seat
            same = (section == s) & (tm == source_tm) & (mp == tm)

            @pl.when(jnp.logical_not(same))
            def _():
                pl.semaphore_signal(
                    barrier, inc=1, device_id=(s, source_tm, tm), device_id_type=MESH
                )
    enc_load.wait()
    up_load.wait()
    hidden_units = gelu(
        dot_nn(normed(enc_ref[...].astype(F32)).astype(BF16), up_ref[...])
    ).astype(BF16)
    row = lax.broadcasted_iota(jnp.int32, (256, 256), 0)
    place = lax.broadcasted_iota(jnp.int32, (256, 256), 1)
    origin = lax.rem(row, 32) * 8 + lax.div(lax.rem(row, 128), 32) * 2 + lax.div(row, 128)
    order = jnp.where(place == origin, 1.0, 0.0).astype(BF16)
    inner[...] = dot_nn(order, hidden_units).astype(BF16).reshape(2, 128, 640)
    down_load.wait()
    e_core_send[...] = dot_nn(inner[1 - c], down_ref[...]).astype(BF16).reshape(4, 32, 1280)
    pl.semaphore_wait(barrier, jnp.where(tm == mp, 22, 23))

    sends = []

    def launch(copy):
        copy.start()
        sends.append(copy)

    def got(block, sem):
        remote(block, block, sem, sem, partner).wait_recv()

    for d in (2, 1, 3, 0):
        zd = around(z, d)
        launch(remote(e_core_send.at[zd], e_core_recv.at[zd], ec_s.at[d], ec_r.at[d], partner))
    e_own[...] = dot_nn(inner[c], down_ref[...]).reshape(4, 32, 1280)
    for d in (2, 1, 3, 0):
        got(e_core_recv.at[around(z, d)], ec_r.at[d])
        if d > 0:
            zd = around(z, d)
            e_send[d] = (e_own[zd] + e_core_recv[zd].astype(F32)).astype(BF16)
            launch(remote(
                e_send.at[d], e_recv.at[d], e_s.at[d], e_r.at[d], (section, tm, zd * 2 + c)
            ))

    slots = [slot_ref[tm * 2], slot_ref[tm * 2 + 1]]

    def shares(first, second, u):
        near, far = [jnp.where(slot == u, 1.0, 0.0) for slot in slots]
        return (first * near + second * far).astype(BF16)

    hyp_load.wait()
    for piece in range(4):
        rows = pl.ds(piece * 64, 64)
        values = hyp_ref[rows, :].astype(F32)
        scale = lax.rsqrt(jnp.mean(values * values, axis=-1, keepdims=True) + 1e-06)
        dec_n[rows, :] = (values * scale).astype(BF16)
    qp_load.wait()
    queries = dot_nn(dec_n[...], qp_ref[...]).astype(BF16).astype(F32)
    for u in range(8):
        q_send[u] = shares(queries[:128], queries[128:], u)
    for d in range(1, 8):
        peer = lax.rem(tm + d, 8)
        target = (section, peer, mp)
        launch(remote(q_send.at[peer], q_recv.at[tm], q_s.at[d], q_r.at[d], target))
        launch(remote(tgt_ref, t_recv.at[tm], t_s.at[d], t_r.at[d], target))
    q_recv[tm] = q_send[tm]
    t_recv[tm] = tgt_ref[...]

    total = e_own[z] + e_core_recv[z].astype(F32)
    for d in range(1, 4):
        got(e_recv.at[d], e_r.at[d])
        total += e_recv[d].astype(F32)
    row = lax.broadcasted_iota(jnp.int32, (32, 256), 0)
    place = lax.broadcasted_iota(jnp.int32, (32, 256), 1)
    order = jnp.where(place == row * 8 + mp, 1.0, 0.0).astype(BF16)
    states = normed(dot_nn(order, enc_ref[...]) + total).astype(BF16)
    kvp_load.wait()
    kv = dot_nn(states, kvp_ref[...]).astype(BF16)
    x_hi = lax.div(tm, 4)
    for k in range(KVH):
        kv_send[k, :, :HD] = kv[:, k * HD:(k + 1) * HD]
        kv_send[k, :, HD:] = kv[:, (KVH + k) * HD:(KVH + k + 1) * HD]
    kv_copies = []
    for k in range(KVH):
        goal_mp = 4 * (k % 2) + y
        same = (section == k // 2) & (tm == mp) & (mp == goal_mp)
        copy = remote(
            kv_send.at[k], kv_all.at[section, x_hi, y], kv1_s.at[k],
            kv1_r.at[section * 2 + x_hi], (k // 2, mp, goal_mp),
        )
        local = pltpu.make_async_copy(
            kv_send.at[k], kv_all.at[section, x_hi, y], kv1_r.at[section * 2 + x_hi]
        )

        @pl.when(same)
        def _():
            local.start()

        @pl.when(jnp.logical_not(same))
        def _():
            copy.start()

        kv_copies.append((copy, same))

    token = (section * 4 + z) * 16
    mine = pl.ds(pl.multiple_of(c * 2048, 2048), 2048)
    other = pl.ds(pl.multiple_of((1 - c) * 2048, 2048), 2048)
    first = hyp_ref[pl.ds(pl.multiple_of(token, 16), 16), mine].astype(F32)
    second = hyp_ref[pl.ds(pl.multiple_of(128 + token, 16), 16), mine].astype(F32)
    for u in range(8):
        r_send[u] = shares(first, second, u)

    for s in range(2):
        for h in range(2):
            got(kv_all.at[s, h, seat], kv1_r.at[s * 2 + h])
    for d in range(1, 4):
        block = kv_all.at[:, :, seat]
        launch(remote(
            block, block, kv2_s.at[d], kv2_r.at[d],
            (section, tm, quad * 4 + lax.rem(seat + d, 4)),
        ))
    for d in range(1, 8):
        peer = lax.rem(tm + d, 8)
        launch(remote(
            r_send.at[peer], r_recv.at[tm], r_s.at[d], r_r.at[d], (section, peer, mp)
        ))
    r_recv[tm] = r_send[tm]
    for d in range(1, 8):
        source = lax.rem(tm - d + 8, 8)
        got(q_recv.at[source], q_r.at[d])
        got(t_recv.at[source], t_r.at[d])
    q_total = q_recv[0].astype(F32)
    t_total = t_recv[0]
    for u in range(1, 8):
        q_total += q_recv[u].astype(F32)
        t_total += t_recv[u]
    query = q_total.astype(BF16)
    targets[...] = t_total
    for d in range(1, 4):
        got(kv_all.at[:, :, lax.rem(seat - d + 4, 4)], kv2_r.at[d])

    limit = length_ref[tm]
    kv = kv_all[...].reshape(512, 256)
    frame = lax.broadcasted_iota(jnp.int32, (128, 512), 1)
    for h in range(2):
        scores = dot_nt(query[:, h * HD:(h + 1) * HD], kv[:, :HD]) * (1.0 / math.sqrt(HD))
        scores = jnp.where(frame < limit, scores, -jnp.inf)
        peak = jnp.max(scores, axis=-1, keepdims=True)
        weights = jnp.exp(scores - peak)
        weights = (weights / jnp.sum(weights, axis=-1, keepdims=True)).astype(BF16)
        context[:, h * HD:(h + 1) * HD] = dot_nn(weights, kv[:, HD:]).astype(BF16)

    op_load.wait()
    core_send[...] = dot_nn(context[...], op_ref[:, other]).astype(BF16).reshape(2, 4, 16, 2048)
    for d in (2, 1, 3, 0):
        zd = around(z, d)
        launch(remote(
            core_send.at[:, zd], core_recv.at[:, zd], c_s.at[d], c_r.at[d], partner
        ))
    own[...] = dot_nn(context[...], op_ref[:, mine]).reshape(2, 4, 16, 2048)
    for d in (2, 1, 3, 0):
        zd = around(z, d)
        got(core_recv.at[:, zd], c_r.at[d])
        for side in (1, 0):
            if side or d:
                half = lax.rem(section + side, 2)
                n = side * 4 + d
                rs_send[n] = (own[half, zd] + core_recv[half, zd].astype(F32)).astype(BF16)
                launch(remote(
                    rs_send.at[n], rs_recv.at[n], rs_s.at[n], rs_r.at[n], (half, tm, zd * 2 + c)
                ))
    for d in range(1, 8):
        got(r_recv.at[lax.rem(tm - d + 8, 8)], r_r.at[d])
    resid = r_recv[0].astype(F32)
    for u in range(1, 8):
        resid += r_recv[u].astype(F32)
    summed = own[section, z] + core_recv[section, z].astype(F32)
    for n in range(1, 8):
        got(rs_recv.at[n], rs_r.at[n])
        summed += rs_recv[n].astype(F32)
    resid = resid + summed
    squares = jnp.sum(resid * resid, axis=-1, keepdims=True)
    sq_send[...] = jnp.broadcast_to(squares, (16, 128))
    launch(remote(sq_send, sq_recv, sq_s.at[0], sq_r.at[0], partner))
    got(sq_recv, sq_r.at[0])
    total = squares + sq_recv[:, :1]
    hidden[x, y, z, :, mine] = (resid * lax.rsqrt(total * (1.0 / 4096.0) + 1e-06)).astype(BF16)

    def slab(where, start, width, core):
        index = tuple(w if isinstance(w, tuple) else (w, 1) for w in where)
        index = tuple(pl.ds(at, count) for at, count in index)
        column = pl.multiple_of(core * 2048 + start, 128)
        return hidden.at[index[0], index[1], index[2], :, pl.ds(column, width)]

    def place_of(part, stage, q, at):
        order = ORDERS[part]
        where = list(me)
        for axis in order[:stage]:
            where[axis] = (0, 4)
        if q is not None:
            where[order[1]] = around(me[order[1]], q)
        where[order[stage]] = around(me[order[stage]], at)
        return where

    def near_copy(wave, part, stage, step, at):
        block = slab(place_of(part, stage, None, at), *WAVES[wave][part], c)
        n = (wave * 3 + part) * 18 + stage * 3 + STEPS.index(step)
        return remote(block, block, g_s.at[n], g_r.at[n], neighbour(ORDERS[part][stage], step))

    def block_copy(wave, part, q, kind, at):
        block = slab(place_of(part, 2, q, at), *WAVES[wave][part], c)
        n = (wave * 3 + part) * 18 + 6 + QS.index(q) * 3 + kind
        step = (1, -1, 1 if q in UPWARD else -1)[kind]
        return remote(block, block, g_s.at[n], g_r.at[n], neighbour(ORDERS[part][2], step))

    def near_send(wave, stage):
        for step in STEPS:
            for part in range(3):
                launch(near_copy(wave, part, stage, step, 0))

    def near_wait(wave, stage):
        for part in range(3):
            for step in STEPS:
                near_copy(wave, part, stage, step, -step).wait_recv()

    def send(wave, *qs):
        for q in qs:
            for part in range(3):
                launch(block_copy(wave, part, q, 0, 0))
                launch(block_copy(wave, part, q, 1, 0))

    def relay(wave, *qs):
        for q in qs:
            for part in range(3):
                if q in UPWARD:
                    block_copy(wave, part, q, 0, -1).wait_recv()
                    launch(block_copy(wave, part, q, 2, -1))
                    block_copy(wave, part, q, 1, 1).wait_recv()
                else:
                    block_copy(wave, part, q, 1, 1).wait_recv()
                    launch(block_copy(wave, part, q, 2, 1))
                    block_copy(wave, part, q, 0, -1).wait_recv()

    def finish(wave, *qs):
        for q in qs:
            for part in range(3):
                block_copy(wave, part, q, 2, 2).wait_recv()

    def forward_copy(wave, part, at, core):
        start, width = WAVES[wave][part]
        block = slab(place_of(part, 2, None, at), start, width, core)
        n = (wave * 3 + part) * 4 + QS.index(at)
        return remote(block, block, f_s.at[n], f_r.at[n], partner)

    def forward(wave, *ats):
        for at in ats:
            for part in range(3):
                launch(forward_copy(wave, part, at, c))

    def tick(wave, n):
        if n == 0:
            near_send(wave, 0)
        if n == 1:
            near_wait(wave, 0)
            near_send(wave, 1)
            send(wave, 0)
        if n == 2:
            near_wait(wave, 1)
            send(wave, 1, -1, 2)
            forward(wave, 0)
        if n == 3:
            relay(wave, 0)
        if n == 4:
            relay(wave, 1, -1)
        if n == 5:
            relay(wave, 2)
            forward(wave, 1, -1)
        if n == 6:
            finish(wave, *QS)
            forward(wave, 2)

    def arrived(wave):
        for part in range(3):
            for at in QS:
                forward_copy(wave, part, at, 1 - c).wait_recv()

    vocab_rows = head.shape[0]

    def wave_logits(wave, xs):
        total = None
        low, high = WAVES[wave][0][0], sum(WAVES[wave][2])
        for half in range(2):
            cols = slice(half * 2048 + low, half * 2048 + high)
            tokens = hidden[xs, :, :, :, cols].reshape(256, high - low)
            term = dot_nt(head[:, cols], tokens)
            total = term if total is None else total + term
        return total

    for wave, n in SCHEDULE:
        tick(wave, n)
    head_load.wait()
    arrived(0)

    def first(xs):
        lanes = pl.ds(pl.multiple_of(xs * 256, 256), 256)
        acc[:, lanes] = wave_logits(0, xs)

    @pl.loop(0, 2)
    def _(xs):
        first(xs)

    tick(1, 5)

    @pl.loop(2, 4)
    def _(xs):
        first(xs)

    tick(1, 6)
    arrived(1)

    vocab_start = ((section * 8 + tm) * 8 + mp) * vocab_rows

    @pl.loop(0, 4)
    def _(xs):
        lanes = pl.ds(pl.multiple_of(xs * 256, 256), 256)
        logits = acc[:, lanes] + wave_logits(1, xs)
        upper = jnp.max(logits, axis=0, keepdims=True)
        totals = jnp.sum(jnp.exp(logits - upper), axis=0, keepdims=True)
        wanted = jnp.concatenate([targets[pl.ds(xs * 2, 1), :], targets[pl.ds(xs * 2 + 1, 1), :]], 1)
        row = lax.broadcasted_iota(jnp.int32, logits.shape, 0)
        chosen = jnp.sum(
            jnp.where(row == wanted - vocab_start, logits, 0.0), axis=0, keepdims=True
        )
        for n, value in enumerate((upper, totals, chosen)):
            stats[n, pl.ds(xs * 2, 1), :] = value[:, :128]
            stats[n, pl.ds(xs * 2 + 1, 1), :] = value[:, 128:]

    def exchange(buffer, count, my_place, target_of, send_sem, recv_sem):
        copies = []
        for d in range(1, count):
            copy = remote(
                stats, buffer.at[my_place], send_sem.at[d], recv_sem.at[d], target_of(d)
            )
            copy.start()
            copies.append(copy)
        buffer[my_place] = stats[...]
        for d in range(1, count):
            block = buffer.at[lax.rem(my_place - d + count, count)]
            remote(block, block, send_sem.at[d], recv_sem.at[d], partner).wait_recv()
        peak = buffer[0, 0]
        for n in range(1, count):
            peak = jnp.maximum(peak, buffer[n, 0])
        total = buffer[0, 1] * jnp.exp(buffer[0, 0] - peak)
        chosen = buffer[0, 2]
        for n in range(1, count):
            total += buffer[n, 1] * jnp.exp(buffer[n, 0] - peak)
            chosen += buffer[n, 2]
        for copy in copies:
            copy.wait_send()
        stats[0], stats[1], stats[2] = peak, total, chosen

    exchange(all_mp, 8, mp, lambda d: (section, tm, lax.rem(mp + d, 8)), mp_s, mp_r)
    exchange(all_y, 4, y, lambda d: neighbour(1, d), y_s, y_r)
    exchange(all_x, 4, x, lambda d: neighbour(0, d), x_s, x_r)
    out_ref[...] = stats[2] - (stats[0] + jnp.log(stats[1]))
    for copy in sends:
        copy.wait_send()
    for copy, same in kv_copies:

        @pl.when(jnp.logical_not(same))
        def _():
            copy.wait_send()


def vmem():
    return pl.BlockSpec(memory_space=pltpu.VMEM)


def params(collective):
    return pltpu.CompilerParams(
        collective_id=collective, has_side_effects=True, vmem_limit_bytes=VMEM_LIMIT
    )


def dma(*counts):
    return [pltpu.SemaphoreType.DMA((n,)) for n in counts]


def per_device(
    frame_len, slot_utt, enc_in, ffn_up, ffn_down, kv_proj,
    hyp_state, hyp_tok, hyp_len, q_proj, o_proj, head,
):
    tm = lax.axis_index("tm")
    here = lax.dynamic_slice_in_dim(slot_utt, tm * 2, 2, 0)
    utterances = jnp.arange(8, dtype=jnp.int32)
    holds = here[:, None] == utterances[None, :]
    tokens = hyp_tok.reshape(2, 128)
    tiles = jnp.sum(jnp.where(holds[:, :, None], tokens[:, None, :], 0), axis=0)
    tiles = tiles.reshape(2, 4, 2, 64).transpose(0, 2, 1, 3).reshape(8, 128)

    anywhere = pl.BlockSpec(memory_space=pl.ANY)
    smem = pl.BlockSpec(memory_space=pltpu.SMEM)
    logp = pl.pallas_call(
        kernel,
        out_shape=jax.ShapeDtypeStruct((8, 128), F32),
        in_specs=[smem, smem, vmem()] + [anywhere] * 8,
        out_specs=vmem(),
        scratch_shapes=[
            pltpu.VMEM((256, 1280), BF16),
            pltpu.VMEM((1280, 640), BF16),
            pltpu.VMEM((640, 1280), BF16),
            pltpu.VMEM((256, 4096), BF16),
            pltpu.VMEM((4096, 256), BF16),
            pltpu.VMEM((1280, 1024), BF16),
            pltpu.VMEM((256, 4096), BF16),
            pltpu.VMEM(head.shape, BF16),
            pltpu.VMEM((2, 128, 640), BF16),
            pltpu.VMEM((4, 32, 1280), BF16),
            pltpu.VMEM((4, 32, 1280), BF16),
            pltpu.VMEM((4, 32, 1280), F32),
            pltpu.VMEM((4, 32, 1280), BF16),
            pltpu.VMEM((4, 32, 1280), BF16),
            pltpu.VMEM((4, 32, 256), BF16),
            pltpu.VMEM((2, 2, 4, 32, 256), BF16),
            pltpu.VMEM((256, 4096), BF16),
            pltpu.VMEM((8, 128, 256), BF16),
            pltpu.VMEM((8, 128, 256), BF16),
            pltpu.VMEM((8, 16, 2048), BF16),
            pltpu.VMEM((8, 16, 2048), BF16),
            pltpu.VMEM((8, 8, 128), jnp.int32),
            pltpu.VMEM((8, 128), jnp.int32),
            pltpu.VMEM((128, 256), BF16),
            pltpu.VMEM((2, 4, 16, 2048), BF16),
            pltpu.VMEM((2, 4, 16, 2048), BF16),
            pltpu.VMEM((2, 4, 16, 2048), F32),
            pltpu.VMEM((8, 16, 2048), BF16),
            pltpu.VMEM((8, 16, 2048), BF16),
            pltpu.VMEM((16, 128), F32),
            pltpu.VMEM((16, 128), F32),
            pltpu.VMEM((4, 4, 4, 16, 4096), BF16),
            pltpu.VMEM((head.shape[0], 1024), F32),
            pltpu.VMEM((3, 8, 128), F32),
            pltpu.VMEM((8, 3, 8, 128), F32),
            pltpu.VMEM((4, 3, 8, 128), F32),
            pltpu.VMEM((4, 3, 8, 128), F32),
        ]
        + dma(8, 4, 4, 4, 4, 4, 4, 4, 4, 8, 8, 8, 8, 8, 8, 4, 4, 8, 8, 1, 1)
        + dma(108, 108, 24, 24, 8, 8, 4, 4, 4, 4),
        compiler_params=params(1),
        name="rescore",
    )(
        slot_utt, frame_len, tiles, enc_in.reshape(256, 1280), ffn_up, ffn_down,
        hyp_state.reshape(256, 4096), q_proj, kv_proj, o_proj, head,
    )

    by_utt = logp.reshape(2, 2, 4, 64).transpose(0, 2, 1, 3).reshape(8, 128)
    own_logp = jnp.sum(jnp.where(holds[:, :, None], by_utt[None], 0.0), axis=1).reshape(2, 8, 16)
    valid = jnp.arange(16, dtype=jnp.int32)[None, None, :] < hyp_len[:, :, None]
    summed = jnp.sum(jnp.where(valid, own_logp, 0.0), axis=-1) / hyp_len.astype(F32) + math.log(V)
    return jnp.where(here[:, None] >= 0, summed, 0.0)


def solution(mesh):
    in_specs = (
        P(),
        P(),
        P(("section", "tm"), None, None),
        P(None, "mp"),
        P("mp", None),
        P(),
        P("tm", None, None, None),
        P("tm", None, None),
        P("tm", None),
        P(None, ("section", "mp")),
        P(("section", "mp"), None),
        P(("section", "tm", "mp"), None),
    )
    return jax.shard_map(
        per_device, mesh=mesh, in_specs=in_specs, out_specs=P("tm", None), check_vma=False
    )
```
